32 devices in a mesh: ens: 2 (over x), lat: 4 (over y, core), lon: 4 (over z).
Axes of the slice: x: 2, y: 2, z: 4, core: 2. Of those that a mesh axis runs over, the one named last changes fastest.
Arguments:
- starting_state: bfloat16 [4, 222, 128, 512], P('ens', None, 'lat', 'lon'), may hold values from -6 to 6
- random_fields: bfloat16 [4, 16, 128, 512], P('ens', None, 'lat', 'lon'), may hold values from -6 to 6
- observed: float32 [6, 13, 128, 512], P(None, None, 'lat', 'lon'), may hold values from -6 to 6
- input_weight: bfloat16 [256, 222], replicated, may hold values from -0.375 to 0.375
- random_weight: bfloat16 [256, 16], replicated, may hold values from -1.5 to 1.5
- hidden_weight: bfloat16 [256, 256], replicated, may hold values from -0.375 to 0.375
- output_weight: bfloat16 [222, 256], replicated, may hold values from -0.375 to 0.375
- diffusivity: float32 [222], replicated, may hold values from 0.02 to 0.24
Outputs:
- grad_state: bfloat16 [4, 222, 128, 512], P('ens', None, 'lat', 'lon')
- grad_w_in: float32 [256, 222], replicated
- grad_w_noise: float32 [256, 16], replicated
- grad_w_mid: float32 [256, 256], replicated
- grad_w_out: float32 [222, 256], replicated
- grad_diffusivity: float32 [222], replicated
The draws below stay inside these ranges and needn't reach their ends.
All inputs are finite; a program needn't handle non-finite values.
Results may differ from the reference program's by a relative error of at most 0.008.
Values may be sent and summed in bfloat16 or wider, within the bound.
No kernel may reach another device: no remote copies, remote signals or barrier semaphores. Data moves between devices by JAX's collectives and lax.ppermute only.
A program may use at most 128 MiB of HBM per device.

```python
import math
import jax
import jax.numpy as jnp
from jax import lax

PROGNOSTIC_COUNT = 6
LEVEL_COUNT = 37
HID = 256
NOISE = 16
CHANNELS = 222
SCORED = 13
MEMBER_COUNT = 4
LATITUDE_ROWS = 128
LONGITUDE_COLUMN = 512


def levels(rng, extent, shards, least, high):
    def one(position, parts):
        heights = jax.random.uniform(jax.random.fold_in(jax.random.fold_in(rng, 6), position), (parts,), jnp.float32, least / len(shards), high / len(shards))
        return jnp.repeat(jnp.exp(heights), extent[position] // parts).reshape((-1,) + (1,) * (len(extent) - position - 1))

    level = one(*shards[0])
    for cut in shards[1:]:
        level = level * one(*cut)
    return level


def centred(rng, dims, width, reach, split=(), dtype=jnp.bfloat16):
    values = jax.random.normal(rng, dims, jnp.float32) * width
    if len(split) > 0:
        values = levels(rng, dims, split, -0.22, 0.18) * values
    return jnp.clip(values, min=-reach, max=reach).astype(dtype)


def setup_inputs(seed: int = 0) -> dict:
    arg_keys = jax.random.split(jax.random.key(seed), 9)
    return {
        "starting_state": centred(arg_keys[0], (MEMBER_COUNT, CHANNELS, LATITUDE_ROWS, LONGITUDE_COLUMN), 1.0, 6.0, ((0, 2), (2, 4), (3, 4))),
        "random_fields": centred(arg_keys[1], (MEMBER_COUNT, NOISE, LATITUDE_ROWS, LONGITUDE_COLUMN), 1.0, 6.0, ((0, 2), (2, 4), (3, 4))),
        "observed": centred(arg_keys[2], (PROGNOSTIC_COUNT, SCORED, LATITUDE_ROWS, LONGITUDE_COLUMN), 1.0, 6.0, ((2, 4), (3, 4)), jnp.float32),
        "input_weight": centred(arg_keys[3], (HID, CHANNELS), CHANNELS ** -0.5, 0.375),
        "random_weight": centred(arg_keys[4], (HID, NOISE), NOISE ** -0.5, 1.5),
        "hidden_weight": centred(arg_keys[5], (HID, HID), HID ** -0.5, 0.375),
        "output_weight": centred(arg_keys[6], (CHANNELS, HID), HID ** -0.5, 0.375),
        "diffusivity": jnp.clip(jnp.exp(jax.random.uniform(arg_keys[7], (CHANNELS,), jnp.float32, math.log(0.02), math.log(0.24))), 0.02, 0.24),
    }


DELTA = 0.1

def softened_slope(diff):
    return diff * lax.rsqrt(diff * diff + DELTA * DELTA)

def silu_slope(value):
    gate = jax.nn.sigmoid(value)
    return gate * (1.0 + value * (1.0 - gate))

def laplace(field):
    zero_row = jnp.zeros_like(field[:, :1, :])
    north = jnp.concatenate([field[:, 1:, :], zero_row], axis=1)
    south = jnp.concatenate([zero_row, field[:, :-1, :]], axis=1)
    return north + south + jnp.roll(field, 1, axis=2) + jnp.roll(field, -1, axis=2) - 4.0 * field

def forward_member(single_state, single_random_field, input_weight, random_weight, hidden_weight, output_weight, diffusivity):
    start = single_state.astype(jnp.float32)
    laplacian_initial = laplace(start)
    stepped = start + diffusivity[:, None, None] * laplacian_initial
    advanced_partner = stepped.astype(jnp.bfloat16).reshape(CHANNELS, LATITUDE_ROWS * LONGITUDE_COLUMN)
    random_flattened = single_random_field.reshape(NOISE, LATITUDE_ROWS * LONGITUDE_COLUMN)
    first_preactivation = jnp.dot(input_weight, advanced_partner, preferred_element_type=jnp.float32) + jnp.dot(random_weight, random_flattened, preferred_element_type=jnp.float32)
    first_activation = jax.nn.silu(first_preactivation).astype(jnp.bfloat16)
    second_preactivation = jnp.dot(hidden_weight, first_activation, preferred_element_type=jnp.float32)
    second_activation = jax.nn.silu(second_preactivation).astype(jnp.bfloat16)
    complete_state = stepped.reshape(CHANNELS, LATITUDE_ROWS * LONGITUDE_COLUMN) + jnp.dot(output_weight, second_activation, preferred_element_type=jnp.float32)
    member_prediction = complete_state.reshape(PROGNOSTIC_COUNT, LEVEL_COUNT, LATITUDE_ROWS * LONGITUDE_COLUMN)[:, ::3].astype(jnp.bfloat16)
    return (member_prediction, laplacian_initial, advanced_partner, random_flattened, first_preactivation, first_activation, second_preactivation, second_activation)

def reference(starting_state, random_fields, observed, input_weight, random_weight, hidden_weight, output_weight, diffusivity):

    def forward_without_gradient(pair):
        return forward_member(pair[0], pair[1], input_weight, random_weight, hidden_weight, output_weight, diffusivity)[0]
    member_predictions = lax.map(forward_without_gradient, (starting_state, random_fields)).astype(jnp.float32)
    observed_target = observed.reshape(PROGNOSTIC_COUNT, SCORED, LATITUDE_ROWS * LONGITUDE_COLUMN)

    def accumulate_member(member_index, overall_sum):
        partner_member = lax.dynamic_index_in_dim(member_predictions, member_index, 0, keepdims=False)
        return overall_sum + softened_slope(member_predictions - partner_member)
    pairwise_sum = lax.fori_loop(0, MEMBER_COUNT, accumulate_member, jnp.zeros_like(member_predictions))
    score_gradient = (softened_slope(member_predictions - observed_target[None]) - pairwise_sum / (MEMBER_COUNT - 1.0)).astype(jnp.bfloat16)
    w_out_scored = output_weight.reshape(PROGNOSTIC_COUNT, LEVEL_COUNT, HID)[:, ::3].reshape(PROGNOSTIC_COUNT * SCORED, HID)

    def backward_one(triple):
        single_state, single_random_field, grad_one = triple
        member_prediction, laplacian_initial, advanced_partner, random_flattened, first_preactivation, first_activation, second_preactivation, second_activation = forward_member(single_state, single_random_field, input_weight, random_weight, hidden_weight, output_weight, diffusivity)
        grad_flat = grad_one.reshape(PROGNOSTIC_COUNT * SCORED, LATITUDE_ROWS * LONGITUDE_COLUMN)
        out_term = jnp.dot(grad_flat, second_activation.T, preferred_element_type=jnp.float32)
        back_second = jnp.dot(w_out_scored.T, grad_flat, preferred_element_type=jnp.float32)
        delta_second = (back_second * silu_slope(second_preactivation)).astype(jnp.bfloat16)
        mid_term = jnp.dot(delta_second, first_activation.T, preferred_element_type=jnp.float32)
        back_first = jnp.dot(hidden_weight.T, delta_second, preferred_element_type=jnp.float32)
        delta_first = (back_first * silu_slope(first_preactivation)).astype(jnp.bfloat16)
        in_term = jnp.dot(delta_first, advanced_partner.T, preferred_element_type=jnp.float32)
        noise_term = jnp.dot(delta_first, random_flattened.T, preferred_element_type=jnp.float32)
        grad_stepped = jnp.dot(input_weight.T, delta_first, preferred_element_type=jnp.float32)
        grad_stepped = grad_stepped.reshape(PROGNOSTIC_COUNT, LEVEL_COUNT, LATITUDE_ROWS * LONGITUDE_COLUMN).at[:, ::3].add(grad_one.astype(jnp.float32))
        grad_stepped = grad_stepped.reshape(CHANNELS, LATITUDE_ROWS, LONGITUDE_COLUMN)
        diffusivity_term = lax.optimization_barrier(jnp.sum(grad_stepped * laplacian_initial, axis=(1, 2)))
        grad_state = (grad_stepped + diffusivity[:, None, None] * laplace(grad_stepped)).astype(jnp.bfloat16)
        return (grad_state, in_term, noise_term, mid_term, out_term, diffusivity_term)
    grad_state, in_terms, noise_terms, mid_terms, out_terms, diffusivity_terms = lax.map(backward_one, (starting_state, random_fields, score_gradient))
    inverse_count = 1.0 / (MEMBER_COUNT * LATITUDE_ROWS * LONGITUDE_COLUMN)
    out_scored = lax.optimization_barrier(jnp.sum(out_terms, axis=0)).reshape(PROGNOSTIC_COUNT, SCORED, HID)
    grad_w_out = jnp.zeros((PROGNOSTIC_COUNT, LEVEL_COUNT, HID), jnp.float32).at[:, ::3].set(out_scored).reshape(CHANNELS, HID)
    return (grad_state, lax.optimization_barrier(jnp.sum(in_terms, axis=0)) * inverse_count, lax.optimization_barrier(jnp.sum(noise_terms, axis=0)) * inverse_count, lax.optimization_barrier(jnp.sum(mid_terms, axis=0)) * inverse_count, grad_w_out * inverse_count, lax.optimization_barrier(jnp.sum(diffusivity_terms, axis=0)) * inverse_count)
```

```python
import functools

import jax
import jax.numpy as jnp
import numpy as np
from jax import lax
from jax.experimental import pallas as pl
from jax.experimental.pallas import tpu as pltpu
from jax.sharding import PartitionSpec as P


PROGNOSTIC_COUNT = 6
LEVEL_COUNT = 37
SCORED = 13
DELTA = 0.1
SUB = 8

F32 = jnp.float32
BF16 = jnp.bfloat16


def round_up(value, step):
    return -(-value // step) * step


def channel_order():
    return [
        v * LEVEL_COUNT + level
        for first in range(3)
        for v in range(PROGNOSTIC_COUNT)
        for level in range(first, LEVEL_COUNT, 3)
    ]


def nt(a, b, **kw):
    return lax.dot_general(a, b, (((1,), (1,)), ((), ())), preferred_element_type=F32, **kw)


def tn(a, b, **kw):
    return lax.dot_general(a, b, (((0,), (0,)), ((), ())), preferred_element_type=F32, **kw)


def nn(a, b, **kw):
    return lax.dot_general(a, b, (((1,), (0,)), ((), ())), preferred_element_type=F32, **kw)


def softened_slope(diff):
    return diff * lax.rsqrt(diff * diff + DELTA * DELTA)


def params(**kw):
    return pltpu.CompilerParams(vmem_limit_bytes=48 << 20, **kw)


def put_edges(edge_ref, value, place, lanes):
    moved = pltpu.roll(value, place, axis=1)
    before = lax.rem(place + lanes - 1, lanes)
    lane = lax.broadcasted_iota(jnp.int32, value.shape, 1)
    edge_ref[...] = jnp.where((lane == place) | (lane == before), moved, edge_ref[...])


def transpose_kernel(order, channels, st_ref, rf_ref, t_ref, lo_ref, hi_ref, edge_ref, nat, edge):
    m, rb = pl.program_id(0), pl.program_id(1)
    state_rows = lo_ref.shape[1]
    noise = rf_ref.shape[1]
    lanes = st_ref.shape[3]
    span = 2 * SUB * pl.num_programs(1)

    @pl.when((m == 0) & (rb == 0))
    def _():
        edge[...] = jnp.zeros_like(edge)
        nat[channels * SUB : state_rows * SUB, :] = jnp.zeros(
            ((state_rows - channels) * SUB, lanes), F32
        )

    for place, c in enumerate(order):
        nat[place * SUB : (place + 1) * SUB, :] = st_ref[0, c].astype(F32)
    for k in range(noise):
        place = state_rows + k
        nat[place * SUB : (place + 1) * SUB, :] = rf_ref[0, k].astype(F32)
    for s in range(SUB):
        row = nat[pl.ds(s, state_rows + noise, stride=SUB), :]
        t_ref[0, s] = row.astype(BF16)
        put_edges(edge, row[:state_rows], m * span + 2 * (rb * SUB + s), lanes)

    @pl.when(rb == 0)
    def _():
        lo_ref[0] = t_ref[0, 0, :state_rows]

    @pl.when(rb == pl.num_programs(1) - 1)
    def _():
        hi_ref[0] = t_ref[0, SUB - 1, :state_rows]

    edge_ref[...] = edge[...].astype(BF16)


def observed_kernel(scored, obs_ref, out_ref, nat):
    rows = out_ref.shape[1]
    nat[scored * SUB :, :] = jnp.zeros(((rows - scored) * SUB, nat.shape[1]), F32)
    for c in range(scored):
        nat[c * SUB : (c + 1) * SUB, :] = obs_ref[c]
    for s in range(SUB):
        out_ref[s] = nat[pl.ds(s, rows, stride=SUB), :]


def stencil_rows(load, edge_ref, coef_ref, base, rows, block, store):
    state_rows, lanes = coef_ref.shape
    lane = lax.broadcasted_iota(jnp.int32, (block, lanes), 1)
    for c in range(0, state_rows, block):
        edges = edge_ref[c : c + block, :].astype(F32)
        above, here = load(-1, c), load(0, c)
        for i in range(rows):
            below = load(i + 1, c)
            side = pltpu.roll(edges, lax.rem(2 * lanes - base - 2 * i, lanes), axis=1)
            left = jnp.where(lane == 0, side, pltpu.roll(here, 1, axis=1))
            right = jnp.where(lane == lanes - 1, side, pltpu.roll(here, lanes - 1, axis=1))
            lap = above + below + left + right - 4.0 * here
            store(i, c, here, lap, coef_ref[c : c + block, :])
            above, here = here, below


def gate_of(value):
    return 0.5 * jnp.tanh(0.5 * value) + 0.5


def forward_kernel(
    first_row, scored, member_span, cur_ref, up_ref, dn_ref, edge_ref, coef_ref, win_ref, wmid_ref,
    wout_ref, f_ref, x_ref, lap_ref, act1_ref, slope1_ref, act2_ref, slope2_ref, keep,
):
    m = pl.program_id(0)
    state_rows, lanes = coef_ref.shape
    rows = cur_ref.shape[1]
    total = cur_ref.shape[2]
    kept = keep.shape[0]
    block = 32

    def load(i, c):
        if i < 0:
            return up_ref[0, 0, c : c + block, :].astype(F32)
        if i == rows:
            return dn_ref[0, 0, c : c + block, :].astype(F32)
        return cur_ref[0, i, c : c + block, :].astype(F32)

    def store(i, c, here, lap, coef):
        stepped = here + coef * lap
        at = i * lanes
        x_ref[0, c : c + block, at : at + lanes] = stepped.astype(BF16)
        lap_ref[0, i, c : c + block, :] = lap.astype(BF16)
        if c < kept:
            end = min(c + block, kept)
            keep[c:end, at : at + lanes] = stepped[: end - c]

    stencil_rows(
        load, edge_ref, coef_ref, m * member_span + 2 * first_row, rows, block, store
    )
    for i in range(rows):
        x_ref[0, state_rows:, i * lanes : (i + 1) * lanes] = cur_ref[0, i, state_rows:, :]
    width = min(4, rows) * lanes
    scored_row = lax.broadcasted_iota(jnp.int32, (kept, lanes), 0) < scored
    for at in range(0, rows * lanes, width):
        cols = slice(at, at + width)
        pre1 = nn(win_ref[...], x_ref[0, :, cols])
        gate1 = gate_of(pre1)
        act1 = pre1 * gate1
        act1_ref[0, :, cols] = act1.astype(BF16)
        slope1_ref[0, :, cols] = (gate1 + act1 * (1.0 - gate1)).astype(BF16)
        pre2 = nn(wmid_ref[...], act1_ref[0, :, cols])
        gate2 = gate_of(pre2)
        act2 = pre2 * gate2
        act2_ref[0, :, cols] = act2.astype(BF16)
        slope2_ref[0, :, cols] = (gate2 + act2 * (1.0 - gate2)).astype(BF16)
        out = nn(wout_ref[...], act2_ref[0, :, cols]) + keep[:, cols]
        for j in range(width // lanes):
            piece = out[:, j * lanes : (j + 1) * lanes]
            f_ref[0, at // lanes + j] = jnp.where(scored_row, piece, 0.0).astype(BF16)


def backward_kernel(
    partners, first, last, first_row, spread, place_ref, own_ref, *refs
):
    other_refs = refs[:partners]
    (
        obs_ref, x_ref, lap_ref, act1_ref, slope1_ref, act2_ref, slope2_ref, win_ref, wmid_ref, wout_ref,
    ) = refs[partners : partners + 10]
    refs = refs[partners + 10 :]
    in_refs = ()
    if not first:
        in_refs, refs = refs[:5], refs[5:]
    grad_ref, *acc_refs = refs[:6]
    refs = refs[6:]
    if last:
        pack_ref, refs = refs[0], refs[1:]
    score, edge = refs
    step = pl.program_id(0)
    members, rows = own_ref.shape[0], own_ref.shape[1]
    kept, lanes = own_ref.shape[2], own_ref.shape[3]
    total_members = members * (partners + 1)
    state_rows = lap_ref.shape[2]
    in_acc, mid_acc, out_acc, diff_acc, edge_out = acc_refs

    @pl.when(step == 0)
    def _():
        if first:
            for ref in (in_acc, mid_acc, out_acc, diff_acc):
                ref[...] = jnp.zeros_like(ref)
            edge[...] = jnp.zeros_like(edge)
        else:
            for ref, old in zip((in_acc, mid_acc, out_acc, diff_acc), in_refs[:4], strict=True):
                ref[...] = old[...]
            edge[...] = in_refs[4][...].astype(F32)

    for i in range(rows):
        target = obs_ref[i]
        own = [own_ref[m, i].astype(F32) for m in range(members)]
        pairs = [jnp.zeros_like(target) for _ in range(members)]
        for m in range(members):
            for k in range(m + 1, members):
                slope = softened_slope(own[m] - own[k])
                pairs[m] = pairs[m] + slope
                pairs[k] = pairs[k] - slope
            for other in other_refs:
                for k in range(members):
                    pairs[m] = pairs[m] + softened_slope(own[m] - other[k, i].astype(F32))
        for m in range(members):
            grad = softened_slope(own[m] - target) - pairs[m] / (total_members - 1.0)
            score[m, :, i * lanes : (i + 1) * lanes] = grad.astype(BF16)
    diff = diff_acc[...]
    for m in range(members):
        grad = score[m]
        out_acc[...] += nt(grad, act2_ref[m])
        delta2 = (tn(wout_ref[...], grad) * slope2_ref[m].astype(F32)).astype(BF16)
        mid_acc[...] += nt(delta2, act1_ref[m])
        delta1 = (tn(wmid_ref[...], delta2) * slope1_ref[m].astype(F32)).astype(BF16)
        in_acc[...] += nt(delta1, x_ref[m])
        stepped_grad = tn(win_ref[...], delta1)[:state_rows]
        for i in range(rows):
            piece = stepped_grad[:, i * lanes : (i + 1) * lanes]
            top = piece[:kept] + grad[:, i * lanes : (i + 1) * lanes].astype(F32)
            piece = jnp.concatenate([top, piece[kept:]], axis=0)
            diff = diff + piece * lap_ref[m, i].astype(F32)
            grad_ref[m, i] = piece.astype(grad_ref.dtype)
            put_edges(edge, piece, m * spread + 2 * (first_row + step * rows + i), lanes)
    diff_acc[...] = diff

    @pl.when(step == pl.num_programs(0) - 1)
    def _():
        edge_out[...] = edge[...].astype(BF16)
        if last:
            hidden = in_acc.shape[0]
            pack_ref[0:hidden, :] = nn(in_acc[...].astype(BF16), place_ref[...]).astype(BF16)
            pack_ref[hidden : 2 * hidden, :] = mid_acc[...].astype(BF16)
            pack_ref[2 * hidden : 2 * hidden + kept, :] = out_acc[...].astype(BF16)
            row = nt(jnp.ones((8, lanes), F32), diff_acc[...], precision=lax.Precision.HIGHEST)
            row = nn(row.astype(BF16), place_ref[0:state_rows, :])
            pack_ref[2 * hidden + kept : 2 * hidden + kept + 8, :] = row.astype(BF16)
            tail = pack_ref.shape[0] - (2 * hidden + kept + 8)
            pack_ref[2 * hidden + kept + 8 :, :] = jnp.zeros((tail, pack_ref.shape[1]), BF16)


def final_kernel(
    order, member_span, g_ref, up_ref, dn_ref, lo_ref, hi_ref, edge_ref, coef_ref, out_ref, nat
):
    m, rb = pl.program_id(0), pl.program_id(1)
    block = 32
    at_start, at_end = rb == 0, rb == pl.num_programs(1) - 1

    def load(i, c):
        if i < 0:
            inner = up_ref[0, 0, c : c + block, :].astype(F32)
            return jnp.where(at_start, lo_ref[0, c : c + block, :].astype(F32), inner)
        if i == SUB:
            inner = dn_ref[0, 0, c : c + block, :].astype(F32)
            return jnp.where(at_end, hi_ref[0, c : c + block, :].astype(F32), inner)
        return g_ref[0, i, c : c + block, :].astype(F32)

    def store(i, c, here, lap, coef):
        nat[pl.ds(c * SUB + i, block, stride=SUB), :] = here + coef * lap

    stencil_rows(load, edge_ref, coef_ref, m * member_span + 2 * rb * SUB, SUB, block, store)
    for place, c in enumerate(order):
        out_ref[0, c] = nat[place * SUB : (place + 1) * SUB, :].astype(BF16)


def unpack_kernel(
    channels, noise, kept, inverse_count, pack_ref, scat_ref, win_ref, wnoise_ref, mid_ref, out_ref, diff_ref
):
    hidden = win_ref.shape[0]
    first = pack_ref[0:hidden, :].astype(F32) * inverse_count
    win_ref[...] = first[:, :channels]
    wnoise_ref[...] = first[:, channels : channels + noise]
    mid_ref[...] = pack_ref[hidden : 2 * hidden, :].astype(F32) * inverse_count
    scored = pack_ref[2 * hidden : 2 * hidden + kept, :]
    out_ref[...] = nn(scat_ref[...], scored) * inverse_count
    row = pack_ref[2 * hidden + kept : 2 * hidden + kept + 8, :].astype(F32) * inverse_count
    diff_ref[...] = row[0:1, :channels]


def ring(axis, shift):
    count = lax.axis_size(axis)
    return [(i, (i + shift) % count) for i in range(count)]


def reduce_scatter(value, axis):
    count, me = lax.axis_size(axis), lax.axis_index(axis)
    parts = value.reshape(count, value.shape[0] // count, value.shape[1])
    total = lax.dynamic_index_in_dim(parts, me, 0, keepdims=False).astype(F32)
    sent = [
        lax.ppermute(
            lax.dynamic_index_in_dim(parts, lax.rem(me + k, count), 0, keepdims=False),
            axis,
            ring(axis, k),
        )
        for k in range(1, count)
    ]
    for part in sent:
        total = total + part.astype(F32)
    return total.astype(BF16)


def all_sum(value, axis):
    total = value.astype(F32)
    for k in range(1, lax.axis_size(axis)):
        total = total + lax.ppermute(value, axis, ring(axis, k)).astype(F32)
    return total.astype(BF16)


def all_gather(value, axis):
    count, me = lax.axis_size(axis), lax.axis_index(axis)
    out = jnp.zeros((count, *value.shape), value.dtype)
    for k in range(count):
        part = value if k == 0 else lax.ppermute(value, axis, ring(axis, k))
        out = lax.dynamic_update_index_in_dim(out, part, lax.rem(me - k + count, count), 0)
    return out.reshape(count * value.shape[0], value.shape[1])


def lat_halo(low_row, high_row):
    count = lax.axis_size("lat")
    before = lax.ppermute(high_row, "lat", [(i, i + 1) for i in range(count - 1)])
    after = lax.ppermute(low_row, "lat", [(i + 1, i) for i in range(count - 1)])
    return before, after


def lon_halo(edge):
    from_left = lax.ppermute(edge, "lon", ring("lon", 1))
    from_right = lax.ppermute(edge, "lon", ring("lon", -1))
    even = lax.broadcasted_iota(jnp.int32, edge.shape, 1) % 2 == 0
    return jnp.where(even, jnp.roll(from_left, 1, axis=1), jnp.roll(from_right, -1, axis=1))


def on_device(
    starting_state, random_fields, observed, input_weight, random_weight, hidden_weight, output_weight, diffusivity
):
    members, channels, lat_rows, lanes = starting_state.shape
    noise = random_fields.shape[1]
    hidden = hidden_weight.shape[0]
    scored = PROGNOSTIC_COUNT * SCORED
    kept = round_up(scored, 16)
    state_rows = round_up(channels, 32)
    total = state_rows + noise
    span = 2 * lat_rows
    order = channel_order()
    blocks = lat_rows // SUB
    chunk = SUB
    chunks = lat_rows // chunk
    cells = chunk * lanes
    partners = lax.axis_size("ens") - 1
    assert members * span <= lanes and lat_rows % SUB == 0

    place = np.zeros((total, hidden), np.float32)
    for at, c in enumerate(order):
        place[at, c] = 1.0
    for k in range(noise):
        place[state_rows + k, channels + k] = 1.0
    scatter = np.zeros((channels, kept), np.float32)
    for at, c in enumerate(order[:scored]):
        scatter[c, at] = 1.0
    place = jnp.asarray(place, BF16)
    scatter = jnp.asarray(scatter, BF16)
    both = jnp.concatenate([input_weight, random_weight], axis=1)
    w_in = nt(both, place[:, : channels + noise]).astype(BF16)
    w_out = tn(scatter, output_weight).astype(BF16)
    coef = nn(
        place[:state_rows, :channels].astype(F32), diffusivity[:, None], precision=lax.Precision.HIGHEST
    )
    coef = jnp.broadcast_to(coef, (state_rows, lanes))

    whole2 = lambda shape: pl.BlockSpec(shape, lambda *_: (0,) * len(shape))

    rows_t, low, high, edge = pl.pallas_call(
        functools.partial(transpose_kernel, order, channels),
        grid=(members, blocks),
        in_specs=[
            pl.BlockSpec((1, channels, SUB, lanes), lambda m, r: (m, 0, r, 0)),
            pl.BlockSpec((1, noise, SUB, lanes), lambda m, r: (m, 0, r, 0)),
        ],
        out_specs=[
            pl.BlockSpec((1, SUB, total, lanes), lambda m, r: (m, r, 0, 0)),
            pl.BlockSpec((1, state_rows, lanes), lambda m, r: (m, 0, 0)),
            pl.BlockSpec((1, state_rows, lanes), lambda m, r: (m, 0, 0)),
            whole2((state_rows, lanes)),
        ],
        out_shape=[
            jax.ShapeDtypeStruct((members, lat_rows, total, lanes), BF16),
            jax.ShapeDtypeStruct((members, state_rows, lanes), BF16),
            jax.ShapeDtypeStruct((members, state_rows, lanes), BF16),
            jax.ShapeDtypeStruct((state_rows, lanes), BF16),
        ],
        scratch_shapes=[pltpu.VMEM((total * SUB, lanes), F32), pltpu.VMEM((state_rows, lanes), F32)],
        compiler_params=params(),
        name="transpose",
    )(starting_state, random_fields)
    before, after = lat_halo(low, high)
    sides = lon_halo(edge)

    target = pl.pallas_call(
        functools.partial(observed_kernel, scored),
        grid=(blocks,),
        in_specs=[pl.BlockSpec((scored, SUB, lanes), lambda r: (0, r, 0))],
        out_specs=pl.BlockSpec((SUB, kept, lanes), lambda r: (r, 0, 0)),
        out_shape=jax.ShapeDtypeStruct((lat_rows, kept, lanes), F32),
        scratch_shapes=[pltpu.VMEM((kept * SUB, lanes), F32)],
        compiler_params=params(),
        name="observed",
    )(observed.reshape(scored, lat_rows, lanes))

    def forward(index):
        first_row = index * chunk
        row_spec = lambda row: pl.BlockSpec((1, 1, total, lanes), lambda m: (m, row, 0, 0))
        edge_row = pl.BlockSpec((1, 1, state_rows, lanes), lambda m: (m, 0, 0, 0))
        up = (before[:, None], edge_row) if index == 0 else (rows_t, row_spec(first_row - 1))
        down = (after[:, None], edge_row) if index == chunks - 1 else (rows_t, row_spec(first_row + chunk))
        wide = lambda height: pl.BlockSpec((1, height, cells), lambda m: (m, 0, 0))
        return pl.pallas_call(
            functools.partial(forward_kernel, first_row, scored, span),
            grid=(members,),
            in_specs=[
                pl.BlockSpec((1, chunk, total, lanes), lambda m: (m, index, 0, 0)),
                up[1],
                down[1],
                whole2((state_rows, lanes)),
                whole2((state_rows, lanes)),
                whole2((hidden, total)),
                whole2((hidden, hidden)),
                whole2((kept, hidden)),
            ],
            out_specs=[
                pl.BlockSpec((1, chunk, kept, lanes), lambda m: (m, 0, 0, 0)),
                wide(total),
                pl.BlockSpec((1, chunk, state_rows, lanes), lambda m: (m, 0, 0, 0)),
                *[wide(hidden) for _ in range(4)],
            ],
            out_shape=[
                jax.ShapeDtypeStruct((members, chunk, kept, lanes), BF16),
                jax.ShapeDtypeStruct((members, total, cells), BF16),
                jax.ShapeDtypeStruct((members, chunk, state_rows, lanes), BF16),
                *[jax.ShapeDtypeStruct((members, hidden, cells), BF16) for _ in range(4)],
            ],
            scratch_shapes=[pltpu.VMEM((kept, cells), F32)],
            compiler_params=params(),
            name=f"forward{index}",
        )(rows_t, up[0], down[0], sides, coef, w_in, hidden_weight, w_out)

    lat_n, lon_n = lax.axis_size("lat"), lax.axis_size("lon")
    pack_rows = round_up(2 * hidden + kept + 8, 8 * lat_n * lon_n)

    def backward(index, residuals, others, carried):
        own, x, lap, act1, slope1, act2, slope2 = residuals
        first, last = index == 0, index == chunks - 1
        rows = 4
        wide = lambda height: pl.BlockSpec((members, height, rows * lanes), lambda r: (0, 0, r))
        tall = lambda height: pl.BlockSpec((members, rows, height, lanes), lambda r: (0, r, 0, 0))
        steps = chunk // rows
        accs = [(hidden, total), (hidden, hidden), (kept, hidden), (state_rows, lanes), (state_rows, lanes)]
        acc_types = [F32, F32, F32, F32, BF16]
        acc_shapes = [jax.ShapeDtypeStruct(s, t) for s, t in zip(accs, acc_types, strict=True)]
        return pl.pallas_call(
            functools.partial(backward_kernel, partners, first, last, index * chunk, span),
            grid=(steps,),
            in_specs=[
                whole2((total, hidden)),
                *[tall(kept) for _ in range(partners + 1)],
                pl.BlockSpec((rows, kept, lanes), lambda r: (index * steps + r, 0, 0)),
                wide(total),
                tall(state_rows),
                *[wide(hidden) for _ in range(4)],
                whole2((hidden, total)),
                whole2((hidden, hidden)),
                whole2((kept, hidden)),
                *([] if first else [whole2(s) for s in accs]),
            ],
            out_specs=[
                tall(state_rows),
                *[whole2(s) for s in accs],
                *([whole2((pack_rows, hidden))] if last else []),
            ],
            out_shape=[
                jax.ShapeDtypeStruct((members, chunk, state_rows, lanes), F32),
                *acc_shapes,
                *([jax.ShapeDtypeStruct((pack_rows, hidden), BF16)] if last else []),
            ],
            scratch_shapes=[
                pltpu.VMEM((members, kept, rows * lanes), BF16),
                pltpu.VMEM((state_rows, lanes), F32),
            ],
            compiler_params=params(),
            name=f"backward{index}",
        )(
            place, own, *others, target, x, lap, act1, slope1, act2, slope2, w_in, hidden_weight, w_out, *carried
        )

    saved, received = [], []
    for index in range(chunks):
        saved.append(forward(index))
        received.append(
            [lax.ppermute(saved[-1][0], "ens", ring("ens", k)) for k in range(1, partners + 1)]
        )
    grads, carried = [], []
    for index in range(chunks):
        grad, *carried = backward(index, saved[index], received[index], carried)
        grads.append(grad)
    *_, edge, packed = carried

    last_row = grads[-1][:, -1].astype(BF16)
    before, after = lat_halo(grads[0][:, 0].astype(BF16), last_row)
    sides = lon_halo(edge)
    grad = jnp.concatenate(grads, axis=1)
    grad_state = pl.pallas_call(
        functools.partial(final_kernel, order, span),
        grid=(members, blocks),
        in_specs=[
            pl.BlockSpec((1, SUB, state_rows, lanes), lambda m, r: (m, r, 0, 0)),
            pl.BlockSpec((1, 1, state_rows, lanes), lambda m, r: (m, jnp.maximum(r * SUB - 1, 0), 0, 0)),
            pl.BlockSpec(
                (1, 1, state_rows, lanes), lambda m, r: (m, jnp.minimum(r * SUB + SUB, lat_rows - 1), 0, 0)
            ),
            pl.BlockSpec((1, state_rows, lanes), lambda m, r: (m, 0, 0)),
            pl.BlockSpec((1, state_rows, lanes), lambda m, r: (m, 0, 0)),
            whole2((state_rows, lanes)),
            whole2((state_rows, lanes)),
        ],
        out_specs=pl.BlockSpec((1, channels, SUB, lanes), lambda m, r: (m, 0, r, 0)),
        out_shape=jax.ShapeDtypeStruct(starting_state.shape, BF16),
        scratch_shapes=[pltpu.VMEM((state_rows * SUB, lanes), F32)],
        compiler_params=params(),
        name="final",
    )(grad, grad, grad, before, after, sides, coef)

    packed = reduce_scatter(packed, "lat")
    packed = all_sum(packed, "ens")
    packed = reduce_scatter(packed, "lon")
    packed = all_gather(packed, "lon")
    packed = all_gather(packed, "lat")
    count = members * (partners + 1) * lat_rows * lat_n * lanes * lon_n
    g_in, g_noise, g_mid, g_out, g_diff = pl.pallas_call(
        functools.partial(unpack_kernel, channels, noise, kept, 1.0 / count),
        out_shape=[
            jax.ShapeDtypeStruct((hidden, channels), F32),
            jax.ShapeDtypeStruct((hidden, noise), F32),
            jax.ShapeDtypeStruct((hidden, hidden), F32),
            jax.ShapeDtypeStruct((channels, hidden), F32),
            jax.ShapeDtypeStruct((1, channels), F32),
        ],
        compiler_params=params(),
        name="unpack",
    )(packed, scatter)
    return grad_state, g_in, g_noise, g_mid, g_out, g_diff.reshape(channels)


def solution(mesh):
    tiles = P("ens", None, "lat", "lon")
    in_specs = (tiles, tiles, P(None, None, "lat", "lon"), P(), P(), P(), P(), P())
    out_specs = (tiles, P(), P(), P(), P(), P())
    return jax.shard_map(on_device, mesh=mesh, in_specs=in_specs, out_specs=out_specs, check_vma=False)
```

```python
import functools

import jax
import jax.numpy as jnp
import numpy as np
from jax import lax
from jax.experimental import pallas as pl
from jax.experimental.pallas import tpu as pltpu
from jax.sharding import PartitionSpec as P


PROGNOSTIC_COUNT = 6
LEVEL_COUNT = 37
SCORED = 13
DELTA = 0.1
SUB = 8

F32 = jnp.float32
BF16 = jnp.bfloat16


def round_up(value, step):
    return -(-value // step) * step


def channel_order():
    return [
        v * LEVEL_COUNT + level
        for first in range(3)
        for v in range(PROGNOSTIC_COUNT)
        for level in range(first, LEVEL_COUNT, 3)
    ]


def nt(a, b, **kw):
    return lax.dot_general(a, b, (((1,), (1,)), ((), ())), preferred_element_type=F32, **kw)


def tn(a, b, **kw):
    return lax.dot_general(a, b, (((0,), (0,)), ((), ())), preferred_element_type=F32, **kw)


def nn(a, b, **kw):
    return lax.dot_general(a, b, (((1,), (0,)), ((), ())), preferred_element_type=F32, **kw)


def softened_slope(diff):
    return diff * lax.rsqrt(diff * diff + DELTA * DELTA)


def params(**kw):
    return pltpu.CompilerParams(vmem_limit_bytes=10 << 20, **kw)


def put_edges(edge_ref, value, place, lanes):
    moved = pltpu.roll(value, place, axis=1)
    before = lax.rem(place + lanes - 1, lanes)
    lane = lax.broadcasted_iota(jnp.int32, value.shape, 1)
    edge_ref[...] = jnp.where((lane == place) | (lane == before), moved, edge_ref[...])


def transpose_kernel(order, channels, weights, st_ref, rf_ref, *refs):
    sources, (t_ref, lo_ref, hi_ref, edge_ref), prepared = refs[:weights], refs[weights : weights + 4], refs[weights + 4 : -2]
    nat, edge = refs[-2:]
    m, rb = pl.program_id(0), pl.program_id(1)
    state_rows = edge_ref.shape[0]
    noise = rf_ref.shape[1]
    lanes = st_ref.shape[3]
    span = 2 * SUB * pl.num_programs(1)

    @pl.when((m == 0) & (rb == 0))
    def _():
        edge[...] = jnp.zeros_like(edge)
        nat[channels * SUB : state_rows * SUB, :] = jnp.zeros(
            ((state_rows - channels) * SUB, lanes), F32
        )

    for place, c in enumerate(order):
        nat[place * SUB : (place + 1) * SUB, :] = st_ref[0, c].astype(F32)
    for k in range(noise):
        place = state_rows + k
        nat[place * SUB : (place + 1) * SUB, :] = rf_ref[0, k].astype(F32)
    for s in range(SUB):
        row = nat[pl.ds(s, state_rows + noise, stride=SUB), :]
        t_ref[m, rb * SUB + s] = row
        put_edges(edge, row[:state_rows], m * span + 2 * (rb * SUB + s), lanes)

    edge_ref[...] = edge[...].astype(BF16)

    @pl.when((m == pl.num_programs(0) - 1) & (rb == pl.num_programs(1) - 1))
    def _():
        choose_rows(
            t_ref[:, 0, :state_rows], t_ref[:, t_ref.shape[1] - 1, :state_rows], lo_ref, hi_ref
        )
        prepare(*sources, *prepared)


def choose_rows(low, high, first_ref, second_ref):
    even = lax.axis_index("lat") % 2 == 0
    first_ref[...] = jnp.where(even, high, low).astype(BF16)
    second_ref[...] = jnp.where(even, low, high).astype(BF16)


def prepare(
    win_ref, wnoise_ref, wmid_ref, wout_ref, diff_ref, place_ref, placed_ref, scat_ref, shift_ref,
    in_ref, in_half_ref, mid_half_ref, out_ref, out_half_ref, coef_ref,
):
    w_in = tn(win_ref[...], placed_ref[...])
    w_in = w_in + tn(wnoise_ref[...], shift_ref[...])
    in_ref[...] = w_in.astype(BF16)
    in_half_ref[...] = (w_in * 0.5).astype(BF16)
    mid_half_ref[...] = (wmid_ref[...].astype(F32) * 0.5).astype(BF16)
    w_out = tn(scat_ref[...], wout_ref[...])
    out_ref[...] = w_out.astype(BF16)
    out_half_ref[...] = (w_out * 0.5).astype(BF16)
    state_rows, lanes = coef_ref.shape
    spread = jnp.broadcast_to(diff_ref[...], (lanes, diff_ref.shape[1]))
    coef_ref[...] = nt(
        place_ref[:state_rows].astype(F32), spread, precision=lax.Precision.HIGHEST
    )


def observed_kernel(scored, obs_ref, out_ref, nat):
    lat_rows, rows = out_ref.shape[:2]
    nat[scored * SUB :, :] = jnp.zeros(((rows - scored) * SUB, nat.shape[1]), F32)

    def block(rb, _):
        first = pl.multiple_of(rb * SUB, SUB)
        for c in range(scored):
            nat[c * SUB : (c + 1) * SUB, :] = obs_ref[c, pl.ds(first, SUB), :]
        for s in range(SUB):
            out_ref[first + s] = nat[pl.ds(s, rows, stride=SUB), :]
        return 0

    lax.fori_loop(0, lat_rows // SUB, block, 0)


def stencil_setup(left_ref, right_ref, halo, weights):
    lanes = halo.shape[1]
    lane = lax.broadcasted_iota(jnp.int32, halo.shape, 1)
    from_left = pltpu.roll(left_ref[...].astype(F32), 1, axis=1)
    from_right = pltpu.roll(right_ref[...].astype(F32), lanes - 1, axis=1)
    halo[...] = jnp.where(lane % 2 == 0, from_left, from_right)
    k = lax.broadcasted_iota(jnp.int32, (lanes, lanes), 0)
    lane = lax.broadcasted_iota(jnp.int32, (lanes, lanes), 1)
    beside = jnp.where((k == lane + 1) | (k + 1 == lane), 1.0, 0.0) - jnp.where(k == lane, 4.0, 0.0)
    ends = jnp.where((k == lane) & ((k == 0) | (k == lanes - 1)), 1.0, 0.0)
    weights[:lanes, :] = beside.astype(BF16)
    weights[lanes:, :] = ends.astype(BF16)


def stencil_rows(load, halo, weights, base, rows, store):
    lanes = halo.shape[1]
    for i in range(rows):
        turned = pltpu.roll(halo[...], lax.rem(2 * lanes - base - 2 * i, lanes), axis=1)
        row = load(i)
        ends = jnp.concatenate([row.astype(BF16), turned.astype(BF16)], axis=1)
        store(i, row, nn(ends, weights[...]) + load(i - 1) + load(i + 1))


def activate(half):
    gate = jnp.tanh(half)
    part = half * gate
    return half + part, (1.0 + gate) * (1.0 + (half - part))


def forward_kernel(
    first_row, rows, scored, member_span, t_ref, up_ref, dn_ref, left_ref, right_ref, coef_ref, win_ref, wmid_ref,
    wout_ref, f_ref, x_ref, lap_ref, act1_ref, slope1_ref, act2_ref, slope2_ref, keep, around, weights,
):
    state_rows, lanes = coef_ref.shape
    kept = keep.shape[0]
    stencil_setup(left_ref, right_ref, around, weights)
    even = lax.axis_index("lat") % 2 == 0

    def member(m, _):
        def load(i):
            if i < 0 and up_ref is not None:
                return jnp.where(even, up_ref[1][m].astype(F32), up_ref[0][m].astype(F32))
            if i == rows and dn_ref is not None:
                return jnp.where(even, dn_ref[0][m].astype(F32), dn_ref[1][m].astype(F32))
            return t_ref[m, first_row + i, :state_rows, :]

        def store(i, row, lap):
            stepped = row + coef_ref[...] * lap
            at = i * lanes
            x_ref[m, :state_rows, at : at + lanes] = stepped.astype(BF16)
            lap_ref[m, i] = lap.astype(BF16)
            keep[:, at : at + lanes] = stepped[:kept]

        stencil_rows(load, around, weights, m * member_span + 2 * first_row, rows, store)
        for i in range(rows):
            x_ref[m, state_rows:, i * lanes : (i + 1) * lanes] = t_ref[
                m, first_row + i, state_rows:, :
            ].astype(BF16)
        width = min(4, rows) * lanes
        scored_row = lax.broadcasted_iota(jnp.int32, (kept, lanes), 0) < scored
        for at in range(0, rows * lanes, width):
            cols = slice(at, at + width)
            act1, slope1 = activate(nn(win_ref[...], x_ref[m, :, cols]))
            act1_ref[m, :, cols] = act1.astype(BF16)
            slope1_ref[m, :, cols] = slope1.astype(BF16)
            act2, slope2 = activate(nn(wmid_ref[...], act1.astype(BF16)))
            act2_ref[m, :, cols] = act2.astype(BF16)
            slope2_ref[m, :, cols] = slope2.astype(BF16)
            out = nn(wout_ref[...], act2.astype(BF16)) + keep[:, cols]
            for j in range(width // lanes):
                piece = out[:, j * lanes : (j + 1) * lanes]
                f_ref[m, at // lanes + j] = jnp.where(scored_row, piece, 0.0).astype(BF16)
        return 0

    lax.fori_loop(0, t_ref.shape[0], member, 0)


def backward_kernel(
    partners, first, last, first_row, spread, own_ref, *refs
):
    other_refs = refs[:partners]
    (
        obs_ref, x_ref, lap_ref, act1_ref, slope1_ref, act2_ref, slope2_ref, win_ref, wmid_ref, wout_ref,
    ) = refs[partners : partners + 10]
    refs = refs[partners + 10 :]
    in_refs = ()
    if not first:
        in_refs, refs = refs[:6], refs[6:]
    grad_ref, *acc_refs = refs[:6]
    refs = refs[6:]
    if last:
        first_ref, second_ref, refs = refs[0], refs[1], refs[2:]
    score, edge = refs[-2:]
    part_refs = refs[:-2]
    members, chunk_rows, kept, lanes = own_ref.shape
    rows = score.shape[2] // lanes
    total_members = members * (partners + 1)
    state_rows = lap_ref.shape[2]
    in_acc, mid_acc, out_acc, diff_acc, edge_out = acc_refs

    if first:
        for ref in (in_acc, mid_acc, out_acc, diff_acc):
            ref[...] = jnp.zeros_like(ref)
        edge[...] = jnp.zeros_like(edge)
    else:
        for ref, old in zip((in_acc, mid_acc, out_acc, diff_acc), in_refs[:4], strict=True):
            ref[...] = old[...]
        edge[...] = in_refs[4][...].astype(F32)

    def part(step, _):
        for i in range(rows):
            row = step * rows + i
            target = obs_ref[first_row + row]
            own = [own_ref[m, row].astype(F32) for m in range(members)]
            pairs = [jnp.zeros_like(target) for _ in range(members)]
            for m in range(members):
                for k in range(m + 1, members):
                    slope = softened_slope(own[m] - own[k])
                    pairs[m] = pairs[m] + slope
                    pairs[k] = pairs[k] - slope
                for other in other_refs:
                    for k in range(members):
                        pairs[m] = pairs[m] + softened_slope(own[m] - other[k, row].astype(F32))
            for m in range(members):
                grad = softened_slope(own[m] - target) - pairs[m] * (1.0 / (total_members - 1.0))
                score[m, :, i * lanes : (i + 1) * lanes] = grad.astype(BF16)
        diff = diff_acc[...]
        cols = pl.ds(pl.multiple_of(step * (rows * lanes), lanes), rows * lanes)
        for m in range(members):
            grad = score[m]
            out_acc[...] += nt(grad, act2_ref[m, :, cols])
            delta2 = (tn(wout_ref[...], grad) * slope2_ref[m, :, cols].astype(F32)).astype(BF16)
            mid_acc[...] += nt(delta2, act1_ref[m, :, cols])
            delta1 = (tn(wmid_ref[...], delta2) * slope1_ref[m, :, cols].astype(F32)).astype(BF16)
            in_acc[...] += nt(x_ref[m, :, cols], delta1)
            stepped_grad = tn(win_ref[...], delta1)[:state_rows]
            for i in range(rows):
                row = step * rows + i
                piece = stepped_grad[:, i * lanes : (i + 1) * lanes]
                top = piece[:kept] + grad[:, i * lanes : (i + 1) * lanes].astype(F32)
                piece = jnp.concatenate([top, piece[kept:]], axis=0)
                diff = diff + piece * lap_ref[m, row].astype(F32)
                grad_ref[m, first_row + row] = piece
                put_edges(edge, piece, m * spread + 2 * (first_row + row), lanes)
        diff_acc[...] = diff
        return 0

    lax.fori_loop(0, chunk_rows // rows, part, 0)
    edge_out[...] = edge[...].astype(BF16)
    if last:
        low = grad_ref[:, 0] if first else in_refs[5][:, 0]
        choose_rows(low, grad_ref[:, first_row + chunk_rows - 1], first_ref, second_ref)
        pack_ref, part_refs = part_refs[-1], part_refs[:-1]
        at = 0
        for acc in (in_acc, mid_acc, out_acc):
            pack_ref[at : at + acc.shape[0], :] = acc[...].astype(BF16)
            at += acc.shape[0]
        sums = nt(jnp.ones((8, lanes), F32), diff_acc[...], precision=lax.Precision.HIGHEST)
        pack_ref[at:, :] = jnp.zeros((pack_ref.shape[0] - at, pack_ref.shape[1]), BF16)
        pack_ref[at : at + 8, :state_rows] = sums.astype(BF16)
        split_halves(1, pack_ref, *part_refs)


def halves(bit, height):
    mine = lax.axis_index("lat") // bit % 2
    return (pl.ds(pl.multiple_of(side * height, 8), height) for side in (mine, 1 - mine))


def split_halves(bit, value_ref, mine_ref, other_ref):
    mine, other = halves(bit, mine_ref.shape[0])
    mine_ref[...] = value_ref[mine, :]
    other_ref[...] = value_ref[other, :]


def join_halves(bit, mine_ref, other_ref, value_ref):
    mine, other = halves(bit, mine_ref.shape[0])
    value_ref[mine, :] = mine_ref[...]
    value_ref[other, :] = other_ref[...]


def sum_kernel(bit, inputs, *refs):
    total = refs[0][...].astype(F32)
    for ref in refs[1:inputs]:
        total = total + ref[...].astype(F32)
    if bit is None:
        refs[inputs][...] = total.astype(BF16)
    else:
        refs[-1][...] = total.astype(BF16)
        split_halves(bit, refs[-1], *refs[inputs:-1])


def final_kernel(
    order, member_span, rows, first, stride, chunks, g_ref, first_ref, second_ref, left_ref, right_ref, coef_ref, *refs
):
    out_ref, nat, around, weights = refs[-4:]
    m, index = pl.program_id(0), first + pl.program_id(1) * stride
    first_row = index * rows
    state_rows = g_ref.shape[2]
    even = lax.axis_index("lat") % 2 == 0

    @pl.when((m == 0) & (pl.program_id(1) == 0))
    def _():
        stencil_setup(left_ref, right_ref, around, weights)

    def load(i):
        if i < 0:
            halo = jnp.where(even, second_ref[m].astype(F32), first_ref[m].astype(F32))
            return jnp.where(index == 0, halo, g_ref[m, jnp.maximum(first_row - 1, 0)])
        if i == rows:
            inner = g_ref[m, jnp.minimum(first_row + rows, g_ref.shape[1] - 1)]
            halo = jnp.where(even, first_ref[m].astype(F32), second_ref[m].astype(F32))
            return jnp.where(index == chunks - 1, halo, inner)
        return g_ref[m, first_row + i]

    def store(i, row, lap):
        nat[pl.ds(i, state_rows, stride=SUB), :] = row + coef_ref[...] * lap

    stencil_rows(load, around, weights, m * member_span + 2 * first_row, rows, store)
    for place, c in enumerate(order):
        out_ref[0, c] = nat[place * SUB : (place + 1) * SUB, :].astype(BF16)


def unpack_kernel(
    channels, noise, inverse_count, mine_ref, other_ref, place_ref, scat_ref, win_ref, wnoise_ref, mid_ref, out_ref,
    diff_ref, pack_ref,
):
    join_halves(1, mine_ref, other_ref, pack_ref)
    hidden = mid_ref.shape[0]
    total, kept = place_ref.shape[0], scat_ref.shape[1]
    state_rows = total - noise
    win_ref[...] = tn(place_ref[:, :channels], pack_ref[:total, :]) * inverse_count
    wnoise_ref[...] = pack_ref[state_rows:total, :].astype(F32) * inverse_count
    at = total
    mid_ref[...] = pack_ref[at : at + hidden, :].astype(F32) * inverse_count
    at += hidden
    out_ref[...] = nn(scat_ref[...], pack_ref[at : at + kept, :]) * inverse_count
    at += kept
    diff = nn(pack_ref[at : at + 8, :state_rows], place_ref[:state_rows, :channels])
    diff_ref[...] = diff[0:1] * inverse_count


def in_hbm(value):
    return pltpu.with_memory_space_constraint(value, pltpu.HBM)


def in_vmem(value):
    return pltpu.with_memory_space_constraint(value, pltpu.VMEM)


RESIDENT = pl.BlockSpec(memory_space=pltpu.VMEM)


def ring(axis, shift):
    count = lax.axis_size(axis)
    return [(i, (i + shift) % count) for i in range(count)]


def swap(value, start):
    pairs = [(i, i + 1) for i in range(start, lax.axis_size("lat") - 1, 2)]
    return lax.ppermute(value, "lat", [*pairs, *((b, a) for a, b in pairs)])


def across(value, bit):
    return lax.ppermute(value, "lat", [(i, i ^ bit) for i in range(lax.axis_size("lat"))])


def everyone(value, axis):
    return [value, *[lax.ppermute(value, axis, ring(axis, k)) for k in range(1, lax.axis_size(axis))]]


def add_parts(parts, bit=None):
    height, width = parts[0].shape
    count = 1 if bit is None else 2
    return pl.pallas_call(
        functools.partial(sum_kernel, bit, len(parts)),
        in_specs=[RESIDENT] * len(parts),
        out_specs=[RESIDENT] * count,
        out_shape=[pltpu.VMEM((height // count, width), BF16)] * count,
        scratch_shapes=[] if bit is None else [pltpu.VMEM((height, width), BF16)],
        compiler_params=params(),
        name="add_parts",
    )(*map(in_vmem, parts))


def join(bit, mine, other):
    height, width = mine.shape
    return pl.pallas_call(
        functools.partial(join_halves, bit),
        in_specs=[RESIDENT] * 2,
        out_specs=RESIDENT,
        out_shape=pltpu.VMEM((height * 2, width), BF16),
        compiler_params=params(),
        name="join_halves",
    )(in_vmem(mine), in_vmem(other))


def on_device(
    starting_state, random_fields, observed, input_weight, random_weight, hidden_weight, output_weight, diffusivity
):
    members, channels, lat_rows, lanes = starting_state.shape
    noise = random_fields.shape[1]
    hidden = hidden_weight.shape[0]
    scored = PROGNOSTIC_COUNT * SCORED
    kept = round_up(scored, 16)
    state_rows = round_up(channels, 32)
    total = state_rows + noise
    span = 2 * lat_rows
    order = channel_order()
    blocks = lat_rows // SUB
    chunk = SUB
    chunks = lat_rows // chunk
    cells = chunk * lanes
    partners = lax.axis_size("ens") - 1
    assert members * span <= lanes and lat_rows % SUB == 0
    lat_n, lon_n = lax.axis_size("lat"), lax.axis_size("lon")
    assert lat_n > 1 and lat_n & (lat_n - 1) == 0

    place = np.zeros((total, channels), np.float32)
    for at, c in enumerate(order):
        place[at, c] = 1.0
    scatter = np.zeros((channels, kept), np.float32)
    for at, c in enumerate(order[:scored]):
        scatter[c, at] = 1.0
    shift = np.zeros((noise, total), np.float32)
    for k in range(noise):
        shift[k, state_rows + k] = 1.0
    place, placed, scatter, shift = (jnp.asarray(x, BF16) for x in (place, place.T, scatter, shift))
    sources = [
        input_weight.T, random_weight.T, hidden_weight, output_weight, diffusivity.reshape(1, channels),
        place, placed, scatter, shift,
    ]

    whole2 = lambda shape: pl.BlockSpec(shape, lambda *_: (0,) * len(shape))

    rows_t, low, high, edge, w_in, w_in_half, w_mid_half, w_out, w_out_half, coef = pl.pallas_call(
        functools.partial(transpose_kernel, order, channels, len(sources)),
        grid=(members, blocks),
        in_specs=[
            pl.BlockSpec((1, channels, SUB, lanes), lambda m, r: (m, 0, r, 0)),
            pl.BlockSpec((1, noise, SUB, lanes), lambda m, r: (m, 0, r, 0)),
            *[whole2(x.shape) for x in sources],
        ],
        out_specs=[RESIDENT] * 10,
        out_shape=[
            pltpu.VMEM((members, lat_rows, total, lanes), F32),
            pltpu.VMEM((members, state_rows, lanes), BF16),
            pltpu.VMEM((members, state_rows, lanes), BF16),
            pltpu.VMEM((state_rows, lanes), BF16),
            pltpu.VMEM((hidden, total), BF16),
            pltpu.VMEM((hidden, total), BF16),
            pltpu.VMEM((hidden, hidden), BF16),
            pltpu.VMEM((kept, hidden), BF16),
            pltpu.VMEM((kept, hidden), BF16),
            pltpu.VMEM((state_rows, lanes), F32),
        ],
        scratch_shapes=[
            pltpu.VMEM((total * SUB, lanes), F32),
            pltpu.VMEM((state_rows, lanes), F32),
        ],
        compiler_params=params(),
        name="transpose",
    )(in_hbm(starting_state), in_hbm(random_fields), *map(in_hbm, sources))
    sides = [lax.ppermute(edge, "lon", ring("lon", k)) for k in (1, -1)]

    target = pl.pallas_call(
        functools.partial(observed_kernel, scored),
        in_specs=[RESIDENT],
        out_specs=RESIDENT,
        out_shape=pltpu.VMEM((lat_rows, kept, lanes), F32),
        scratch_shapes=[pltpu.VMEM((kept * SUB, lanes), F32)],
        compiler_params=params(),
        name="observed",
    )(in_vmem(observed.reshape(scored, lat_rows, lanes)))

    def forward(index, swapped):
        first_row = index * chunk
        at_start, at_end = index == 0, index == chunks - 1
        halo = list(swapped) if at_start or at_end else []

        def body(t_ref, *refs):
            got, refs = refs[: len(halo)], refs[len(halo) :]
            up, down = got if at_start else None, got if at_end else None
            forward_kernel(first_row, chunk, scored, span, t_ref, up, down, *refs)

        return pl.pallas_call(
            body,
            in_specs=[RESIDENT] * (7 + len(halo)),
            out_specs=[RESIDENT] * 7,
            out_shape=[
                pltpu.VMEM((members, chunk, kept, lanes), BF16),
                pltpu.VMEM((members, total, cells), BF16),
                pltpu.VMEM((members, chunk, state_rows, lanes), BF16),
                *[pltpu.VMEM((members, hidden, cells), BF16) for _ in range(4)],
            ],
            scratch_shapes=[
                pltpu.VMEM((kept, cells), F32),
                pltpu.VMEM((state_rows, lanes), F32),
                pltpu.VMEM((2 * lanes, lanes), BF16),
            ],
            compiler_params=params(),
        )(in_vmem(rows_t), *halo, *sides, coef, w_in_half, w_mid_half, w_out)

    pack_rows = round_up(total + hidden + kept + 8, 16 * lat_n)

    def backward(index, residuals, others, carried, grads):
        own, x, lap, act1, slope1, act2, slope2 = residuals
        first, last = index == chunk_order[0], index == chunk_order[-1]
        rows = 4
        accs = [(total, hidden), (hidden, hidden), (kept, hidden), (state_rows, lanes), (state_rows, lanes)]
        acc_types = [F32, F32, F32, F32, BF16]
        inputs = [
            *map(in_vmem, (own, *others, target, x, lap, act1, slope1, act2, slope2)),
            w_in, w_mid_half, w_out_half, *map(in_vmem, carried), *([] if first else [in_vmem(grads)]),
        ]
        outputs = [
            pltpu.VMEM((members, lat_rows, state_rows, lanes), F32),
            *[pltpu.VMEM(shape, kind) for shape, kind in zip(accs, acc_types, strict=True)],
            *([pltpu.VMEM((members, state_rows, lanes), BF16)] * 2 if last else []),
            *([pltpu.VMEM((pack_rows // 2, hidden), BF16)] * 2 if last else []),
        ]
        return pl.pallas_call(
            functools.partial(backward_kernel, partners, first, last, index * chunk, span),
            in_specs=[RESIDENT] * len(inputs),
            out_specs=[RESIDENT] * len(outputs),
            out_shape=outputs,
            input_output_aliases={} if first else {len(inputs) - 1: 0},
            scratch_shapes=[
                *([pltpu.VMEM((pack_rows, hidden), BF16)] if last else []),
                pltpu.VMEM((members, kept, rows * lanes), BF16),
                pltpu.VMEM((state_rows, lanes), F32),
            ],
            compiler_params=params(),
        )(*inputs)

    chunk_order = [*range(1, chunks - 1), 0, chunks - 1] if chunks > 1 else [0]
    saved, received = {}, {}
    swapped = None
    for index in chunk_order:
        if index == 0:
            swapped = swap(low, 0), swap(high, 1)
        saved[index] = forward(index, swapped)
        received[index] = [
            lax.ppermute(saved[index][0], "ens", ring("ens", k)) for k in range(1, partners + 1)
        ]
    grads, carried = None, []
    for index in chunk_order:
        grads, *carried = backward(index, saved[index], received[index], carried, grads)
        carried, more = carried[:5], carried[5:]
    edge, (low, high, mine, other) = carried[-1], more
    first = swap(low, 0)
    swapped = first, swap(high, 1)
    left = lax.ppermute(edge, "lon", ring("lon", 1))
    sides = left, lax.ppermute(edge, "lon", ring("lon", -1))

    def final(which, out):
        inputs = [*map(in_vmem, (grads, *swapped, *sides)), coef]
        first, stride = which[0], which[-1] - which[0]
        index_map = lambda m, j: (m, 0, first + j * stride, 0)
        return pl.pallas_call(
            functools.partial(final_kernel, order, span, chunk, first, stride, chunks),
            grid=(members, len(which)),
            in_specs=[
                *[RESIDENT] * len(inputs),
                *([] if out is None else [pl.BlockSpec(memory_space=pl.ANY)]),
            ],
            out_specs=pl.BlockSpec((1, channels, chunk, lanes), index_map),
            out_shape=pltpu.HBM(starting_state.shape, BF16),
            scratch_shapes=[
                pltpu.VMEM((state_rows * SUB, lanes), F32),
                pltpu.VMEM((state_rows, lanes), F32),
                pltpu.VMEM((2 * lanes, lanes), BF16),
            ],
            input_output_aliases={} if out is None else {len(inputs): 0},
            compiler_params=params(),
            name="final",
        )(*inputs, *([] if out is None else [out]))

    bits = [1 << k for k in range(lat_n.bit_length() - 1)]
    for bit in bits:
        parts = [mine, across(other, bit)]
        parts = add_parts(parts, None if bit == bits[-1] else 2 * bit)
        mine, other = parts[0], parts[-1]
    parts = everyone(mine, "ens")
    (mine,) = add_parts(parts)
    parts = everyone(mine, "lon")
    grad_state = final(chunk_order[:-2], None)
    (mine,) = add_parts(parts)
    for bit in bits[::-1]:
        other = across(mine, bit)
        if bit != bits[0]:
            mine = join(bit, mine, other)
    parts = [mine, other]
    grad_state = final(chunk_order[-2:], grad_state)
    count = members * (partners + 1) * lat_rows * lat_n * lanes * lon_n
    g_in, g_noise, g_mid, g_out, g_diff = pl.pallas_call(
        functools.partial(unpack_kernel, channels, noise, 1.0 / count),
        out_shape=[
            jax.ShapeDtypeStruct((channels, hidden), F32),
            jax.ShapeDtypeStruct((noise, hidden), F32),
            jax.ShapeDtypeStruct((hidden, hidden), F32),
            jax.ShapeDtypeStruct((channels, hidden), F32),
            jax.ShapeDtypeStruct((1, channels), F32),
        ],
        scratch_shapes=[pltpu.VMEM((pack_rows, hidden), BF16)],
        compiler_params=params(),
        name="unpack",
    )(*map(in_vmem, parts), place, scatter)
    return grad_state, g_in.T, g_noise.T, g_mid, g_out, g_diff.reshape(channels)


def solution(mesh):
    tiles = P("ens", None, "lat", "lon")
    in_specs = (tiles, tiles, P(None, None, "lat", "lon"), P(), P(), P(), P(), P())
    out_specs = (tiles, P(), P(), P(), P(), P())

    return jax.shard_map(on_device, mesh=mesh, in_specs=in_specs, out_specs=out_specs, check_vma=False)
```

```python
import functools

import jax
import jax.numpy as jnp
import numpy as np
from jax import lax
from jax.experimental import pallas as pl
from jax.experimental.pallas import tpu as pltpu
from jax.sharding import PartitionSpec as P


PROGNOSTIC_COUNT = 6
LEVEL_COUNT = 37
SCORED = 13
DELTA = 0.1
SUB = 8

F32 = jnp.float32
BF16 = jnp.bfloat16


def round_up(value, step):
    return -(-value // step) * step


def channel_order():
    return [
        v * LEVEL_COUNT + level
        for first in range(3)
        for v in range(PROGNOSTIC_COUNT)
        for level in range(first, LEVEL_COUNT, 3)
    ]


def nt(a, b, **kw):
    return lax.dot_general(a, b, (((1,), (1,)), ((), ())), preferred_element_type=F32, **kw)


def tn(a, b, **kw):
    return lax.dot_general(a, b, (((0,), (0,)), ((), ())), preferred_element_type=F32, **kw)


def nn(a, b, **kw):
    return lax.dot_general(a, b, (((1,), (0,)), ((), ())), preferred_element_type=F32, **kw)


def softened_slope(diff):
    return diff * lax.rsqrt(diff * diff + DELTA * DELTA)


def params(**kw):
    return pltpu.CompilerParams(vmem_limit_bytes=10 << 20, **kw)


def put_edges(edge_ref, value, place, lanes):
    moved = pltpu.roll(value, place, axis=1)
    before = lax.rem(place + lanes - 1, lanes)
    lane = lax.broadcasted_iota(jnp.int32, value.shape, 1)
    edge_ref[...] = jnp.where((lane == place) | (lane == before), moved, edge_ref[...])


def transpose_kernel(order, channels, weights, st_ref, rf_ref, *refs):
    sources, (t_ref, lo_ref, hi_ref, edge_ref), prepared = refs[:weights], refs[weights : weights + 4], refs[weights + 4 : -2]
    nat, edge = refs[-2:]
    m, rb = pl.program_id(0), pl.program_id(1)
    state_rows = edge_ref.shape[0]
    noise = rf_ref.shape[1]
    lanes = st_ref.shape[3]
    span = 2 * SUB * pl.num_programs(1)

    @pl.when((m == 0) & (rb == 0))
    def _():
        edge[...] = jnp.zeros_like(edge)
        nat[channels * SUB : state_rows * SUB, :] = jnp.zeros(
            ((state_rows - channels) * SUB, lanes), F32
        )

    for place, c in enumerate(order):
        nat[place * SUB : (place + 1) * SUB, :] = st_ref[0, c].astype(F32)
    for k in range(noise):
        place = state_rows + k
        nat[place * SUB : (place + 1) * SUB, :] = rf_ref[0, k].astype(F32)
    for s in range(SUB):
        row = nat[pl.ds(s, state_rows + noise, stride=SUB), :]
        t_ref[m, rb * SUB + s] = row
        put_edges(edge, row[:state_rows], m * span + 2 * (rb * SUB + s), lanes)

    edge_ref[...] = edge[...].astype(BF16)

    @pl.when((m == pl.num_programs(0) - 1) & (rb == pl.num_programs(1) - 1))
    def _():
        choose_rows(
            t_ref[:, 0, :state_rows], t_ref[:, t_ref.shape[1] - 1, :state_rows], lo_ref, hi_ref
        )
        prepare(*sources, *prepared)


def choose_rows(low, high, first_ref, second_ref):
    even = lax.axis_index("lat") % 2 == 0
    first_ref[...] = jnp.where(even, high, low).astype(BF16)
    second_ref[...] = jnp.where(even, low, high).astype(BF16)


def prepare(
    win_ref, wnoise_ref, wmid_ref, wout_ref, diff_ref, place_ref, placed_ref, scat_ref, shift_ref,
    in_ref, in_half_ref, mid_half_ref, out_ref, out_half_ref, coef_ref,
):
    w_in = tn(win_ref[...], placed_ref[...])
    w_in = w_in + tn(wnoise_ref[...], shift_ref[...])
    in_ref[...] = w_in.astype(BF16)
    in_half_ref[...] = (w_in * 0.5).astype(BF16)
    mid_half_ref[...] = (wmid_ref[...].astype(F32) * 0.5).astype(BF16)
    w_out = tn(scat_ref[...], wout_ref[...])
    out_ref[...] = w_out.astype(BF16)
    out_half_ref[...] = (w_out * 0.5).astype(BF16)
    state_rows, lanes = coef_ref.shape
    spread = jnp.broadcast_to(diff_ref[...], (lanes, diff_ref.shape[1]))
    coef_ref[...] = nt(
        place_ref[:state_rows].astype(F32), spread, precision=lax.Precision.HIGHEST
    )


def observed_kernel(scored, obs_ref, out_ref, nat):
    lat_rows, rows = out_ref.shape[:2]
    nat[scored * SUB :, :] = jnp.zeros(((rows - scored) * SUB, nat.shape[1]), F32)

    def block(rb, _):
        first = pl.multiple_of(rb * SUB, SUB)
        for c in range(scored):
            nat[c * SUB : (c + 1) * SUB, :] = obs_ref[c, pl.ds(first, SUB), :]
        for s in range(SUB):
            out_ref[first + s] = nat[pl.ds(s, rows, stride=SUB), :]
        return 0

    lax.fori_loop(0, lat_rows // SUB, block, 0)


def stencil_setup(left_ref, right_ref, halo, weights):
    lanes = halo.shape[1]
    lane = lax.broadcasted_iota(jnp.int32, halo.shape, 1)
    from_left = pltpu.roll(left_ref[...].astype(F32), 1, axis=1)
    from_right = pltpu.roll(right_ref[...].astype(F32), lanes - 1, axis=1)
    halo[...] = jnp.where(lane % 2 == 0, from_left, from_right)
    k = lax.broadcasted_iota(jnp.int32, (lanes, lanes), 0)
    lane = lax.broadcasted_iota(jnp.int32, (lanes, lanes), 1)
    beside = jnp.where((k == lane + 1) | (k + 1 == lane), 1.0, 0.0) - jnp.where(k == lane, 4.0, 0.0)
    ends = jnp.where((k == lane) & ((k == 0) | (k == lanes - 1)), 1.0, 0.0)
    weights[:lanes, :] = beside.astype(BF16)
    weights[lanes:, :] = ends.astype(BF16)


def stencil_rows(load, halo, weights, base, rows, store):
    lanes = halo.shape[1]
    for i in range(rows):
        turned = pltpu.roll(halo[...], lax.rem(2 * lanes - base - 2 * i, lanes), axis=1)
        row = load(i)
        ends = jnp.concatenate([row.astype(BF16), turned.astype(BF16)], axis=1)
        store(i, row, nn(ends, weights[...]) + load(i - 1) + load(i + 1))


def activate(half):
    gate = jnp.tanh(half)
    part = half * gate
    return half + part, (1.0 + gate) * (1.0 + (half - part))


def forward_kernel(
    first_row, rows, scored, member_span, t_ref, up_ref, dn_ref, around, weights, coef_ref, win_ref, wmid_ref,
    wout_ref, f_ref, x_ref, lap_ref, act1_ref, slope1_ref, act2_ref, slope2_ref, keep,
):
    state_rows, lanes = coef_ref.shape
    kept = keep.shape[0]
    even = lax.axis_index("lat") % 2 == 0

    def member(m, _):
        def load(i):
            if i < 0 and up_ref is not None:
                return jnp.where(even, up_ref[1][m].astype(F32), up_ref[0][m].astype(F32))
            if i == rows and dn_ref is not None:
                return jnp.where(even, dn_ref[0][m].astype(F32), dn_ref[1][m].astype(F32))
            return t_ref[m, first_row + i, :state_rows, :]

        def store(i, row, lap):
            stepped = row + coef_ref[...] * lap
            at = i * lanes
            x_ref[m, :state_rows, at : at + lanes] = stepped.astype(BF16)
            lap_ref[m, i] = lap.astype(BF16)
            keep[:, at : at + lanes] = stepped[:kept]

        stencil_rows(load, around, weights, m * member_span + 2 * first_row, rows, store)
        for i in range(rows):
            x_ref[m, state_rows:, i * lanes : (i + 1) * lanes] = t_ref[
                m, first_row + i, state_rows:, :
            ].astype(BF16)
        width = min(4, rows) * lanes
        scored_row = lax.broadcasted_iota(jnp.int32, (kept, lanes), 0) < scored
        for at in range(0, rows * lanes, width):
            cols = slice(at, at + width)
            act1, slope1 = activate(nn(win_ref[...], x_ref[m, :, cols]))
            act1_ref[m, :, cols] = act1.astype(BF16)
            slope1_ref[m, :, cols] = slope1.astype(BF16)
            act2, slope2 = activate(nn(wmid_ref[...], act1.astype(BF16)))
            act2_ref[m, :, cols] = act2.astype(BF16)
            slope2_ref[m, :, cols] = slope2.astype(BF16)
            out = nn(wout_ref[...], act2.astype(BF16)) + keep[:, cols]
            for j in range(width // lanes):
                piece = out[:, j * lanes : (j + 1) * lanes]
                f_ref[m, at // lanes + j] = jnp.where(scored_row, piece, 0.0).astype(BF16)
        return 0

    lax.fori_loop(0, t_ref.shape[0], member, 0, unroll=rows < SUB)


def backward_kernel(
    partners, first, last, first_row, spread, own_ref, *refs
):
    other_refs = refs[:partners]
    (
        obs_ref, x_ref, lap_ref, act1_ref, slope1_ref, act2_ref, slope2_ref, win_ref, wmid_ref, wout_ref,
    ) = refs[partners : partners + 10]
    refs = refs[partners + 10 :]
    in_refs = ()
    if not first:
        in_refs, refs = refs[:6], refs[6:]
    grad_ref, *acc_refs = refs[:6]
    refs = refs[6:]
    if last:
        first_ref, second_ref, refs = refs[0], refs[1], refs[2:]
    score, edge = refs[-2:]
    part_refs = refs[:-2]
    members, chunk_rows, kept, lanes = own_ref.shape
    rows = score.shape[2] // lanes
    total_members = members * (partners + 1)
    state_rows = lap_ref.shape[2]
    in_acc, mid_acc, out_acc, diff_acc, edge_out = acc_refs

    if first:
        for ref in (in_acc, mid_acc, out_acc, diff_acc):
            ref[...] = jnp.zeros_like(ref)
        edge[...] = jnp.zeros_like(edge)
    else:
        for ref, old in zip((in_acc, mid_acc, out_acc, diff_acc), in_refs[:4], strict=True):
            ref[...] = old[...]
        edge[...] = in_refs[4][...].astype(F32)

    def part(step, _):
        for i in range(rows):
            row = step * rows + i
            target = obs_ref[first_row + row]
            own = [own_ref[m, row].astype(F32) for m in range(members)]
            pairs = [jnp.zeros_like(target) for _ in range(members)]
            for m in range(members):
                for k in range(m + 1, members):
                    slope = softened_slope(own[m] - own[k])
                    pairs[m] = pairs[m] + slope
                    pairs[k] = pairs[k] - slope
                for other in other_refs:
                    for k in range(members):
                        pairs[m] = pairs[m] + softened_slope(own[m] - other[k, row].astype(F32))
            for m in range(members):
                grad = softened_slope(own[m] - target) - pairs[m] * (1.0 / (total_members - 1.0))
                score[m, :, i * lanes : (i + 1) * lanes] = grad.astype(BF16)
        diff = diff_acc[...]
        cols = pl.ds(pl.multiple_of(step * (rows * lanes), lanes), rows * lanes)
        for m in range(members):
            grad = score[m]
            out_acc[...] += nt(grad, act2_ref[m, :, cols])
            delta2 = (tn(wout_ref[...], grad) * slope2_ref[m, :, cols].astype(F32)).astype(BF16)
            mid_acc[...] += nt(delta2, act1_ref[m, :, cols])
            delta1 = (tn(wmid_ref[...], delta2) * slope1_ref[m, :, cols].astype(F32)).astype(BF16)
            in_acc[...] += nt(x_ref[m, :, cols], delta1)
            stepped_grad = tn(win_ref[...], delta1)[:state_rows]
            for i in range(rows):
                row = step * rows + i
                piece = stepped_grad[:, i * lanes : (i + 1) * lanes]
                top = piece[:kept] + grad[:, i * lanes : (i + 1) * lanes].astype(F32)
                piece = jnp.concatenate([top, piece[kept:]], axis=0)
                diff = diff + piece * lap_ref[m, row].astype(F32)
                grad_ref[m, first_row + row] = piece
                put_edges(edge, piece, m * spread + 2 * (first_row + row), lanes)
        diff_acc[...] = diff
        return 0

    lax.fori_loop(0, chunk_rows // rows, part, 0)
    edge_out[...] = edge[...].astype(BF16)
    if last:
        choose_rows(in_refs[5][:, 0], in_refs[5][:, grad_ref.shape[1] - 1], first_ref, second_ref)
        pack_ref, part_refs = part_refs[-1], part_refs[:-1]
        at = 0
        for acc in (in_acc, mid_acc, out_acc):
            pack_ref[at : at + acc.shape[0], :] = acc[...].astype(BF16)
            at += acc.shape[0]
        sums = nt(jnp.ones((8, lanes), F32), diff_acc[...], precision=lax.Precision.HIGHEST)
        pack_ref[at:, :] = jnp.zeros((pack_ref.shape[0] - at, pack_ref.shape[1]), BF16)
        pack_ref[at : at + 8, :state_rows] = sums.astype(BF16)
        split_halves(1, pack_ref, *part_refs)


def halves(bit, height):
    mine = lax.axis_index("lat") // bit % 2
    return (pl.ds(pl.multiple_of(side * height, 8), height) for side in (mine, 1 - mine))


def split_halves(bit, value_ref, mine_ref, other_ref):
    mine, other = halves(bit, mine_ref.shape[0])
    mine_ref[...] = value_ref[mine, :]
    other_ref[...] = value_ref[other, :]


def join_halves(bit, mine_ref, other_ref, value_ref):
    mine, other = halves(bit, mine_ref.shape[0])
    value_ref[mine, :] = mine_ref[...]
    value_ref[other, :] = other_ref[...]


def sum_kernel(bit, inputs, *refs):
    total = refs[0][...].astype(F32)
    for ref in refs[1:inputs]:
        total = total + ref[...].astype(F32)
    if bit is None:
        refs[inputs][...] = total.astype(BF16)
    else:
        refs[-1][...] = total.astype(BF16)
        split_halves(bit, refs[-1], *refs[inputs:-1])


def final_kernel(
    order, member_span, rows, first, stride, chunks, g_ref, first_ref, second_ref, left_ref, right_ref, coef_ref, *refs
):
    out_ref, nat, around, weights = refs[-4:]
    m, index = pl.program_id(0), first + pl.program_id(1) * stride
    first_row = index * rows
    state_rows = g_ref.shape[2]
    even = lax.axis_index("lat") % 2 == 0

    @pl.when((m == 0) & (pl.program_id(1) == 0))
    def _():
        stencil_setup(left_ref, right_ref, around, weights)

    def load(i):
        if i < 0:
            halo = jnp.where(even, second_ref[m].astype(F32), first_ref[m].astype(F32))
            return jnp.where(index == 0, halo, g_ref[m, jnp.maximum(first_row - 1, 0)])
        if i == rows:
            inner = g_ref[m, jnp.minimum(first_row + rows, g_ref.shape[1] - 1)]
            halo = jnp.where(even, first_ref[m].astype(F32), second_ref[m].astype(F32))
            return jnp.where(index == chunks - 1, halo, inner)
        return g_ref[m, first_row + i]

    def store(i, row, lap):
        nat[pl.ds(i, state_rows, stride=SUB), :] = row + coef_ref[...] * lap

    stencil_rows(load, around, weights, m * member_span + 2 * first_row, rows, store)
    for place, c in enumerate(order):
        out_ref[0, c] = nat[place * SUB : (place + 1) * SUB, :].astype(BF16)


def unpack_kernel(
    channels, noise, inverse_count, mine_ref, other_ref, place_ref, scat_ref, win_ref, wnoise_ref, mid_ref, out_ref,
    diff_ref, pack_ref,
):
    join_halves(1, mine_ref, other_ref, pack_ref)
    hidden = mid_ref.shape[0]
    total, kept = place_ref.shape[0], scat_ref.shape[1]
    state_rows = total - noise
    win_ref[...] = tn(place_ref[:, :channels], pack_ref[:total, :]) * inverse_count
    wnoise_ref[...] = pack_ref[state_rows:total, :].astype(F32) * inverse_count
    at = total
    mid_ref[...] = pack_ref[at : at + hidden, :].astype(F32) * inverse_count
    at += hidden
    out_ref[...] = nn(scat_ref[...], pack_ref[at : at + kept, :]) * inverse_count
    at += kept
    diff = nn(pack_ref[at : at + 8, :state_rows], place_ref[:state_rows, :channels])
    diff_ref[...] = diff[0:1] * inverse_count


def in_hbm(value):
    return pltpu.with_memory_space_constraint(value, pltpu.HBM)


def in_vmem(value):
    return pltpu.with_memory_space_constraint(value, pltpu.VMEM)


RESIDENT = pl.BlockSpec(memory_space=pltpu.VMEM)


def ring(axis, shift):
    count = lax.axis_size(axis)
    return [(i, (i + shift) % count) for i in range(count)]


def swap(value, start):
    pairs = [(i, i + 1) for i in range(start, lax.axis_size("lat") - 1, 2)]
    return lax.ppermute(value, "lat", [*pairs, *((b, a) for a, b in pairs)])


def across(value, bit):
    return lax.ppermute(value, "lat", [(i, i ^ bit) for i in range(lax.axis_size("lat"))])


def everyone(value, axis):
    return [value, *[lax.ppermute(value, axis, ring(axis, k)) for k in range(1, lax.axis_size(axis))]]


def add_parts(parts, bit=None):
    height, width = parts[0].shape
    count = 1 if bit is None else 2
    return pl.pallas_call(
        functools.partial(sum_kernel, bit, len(parts)),
        in_specs=[RESIDENT] * len(parts),
        out_specs=[RESIDENT] * count,
        out_shape=[pltpu.VMEM((height // count, width), BF16)] * count,
        scratch_shapes=[] if bit is None else [pltpu.VMEM((height, width), BF16)],
        compiler_params=params(),
        name="add_parts",
    )(*map(in_vmem, parts))


def join(bit, mine, other):
    height, width = mine.shape
    return pl.pallas_call(
        functools.partial(join_halves, bit),
        in_specs=[RESIDENT] * 2,
        out_specs=RESIDENT,
        out_shape=pltpu.VMEM((height * 2, width), BF16),
        compiler_params=params(),
        name="join_halves",
    )(in_vmem(mine), in_vmem(other))


def on_device(
    starting_state, random_fields, observed, input_weight, random_weight, hidden_weight, output_weight, diffusivity
):
    members, channels, lat_rows, lanes = starting_state.shape
    noise = random_fields.shape[1]
    hidden = hidden_weight.shape[0]
    scored = PROGNOSTIC_COUNT * SCORED
    kept = round_up(scored, 16)
    state_rows = round_up(channels, 32)
    total = state_rows + noise
    span = 2 * lat_rows
    order = channel_order()
    blocks = lat_rows // SUB
    partners = lax.axis_size("ens") - 1
    assert members * span <= lanes and lat_rows % SUB == 0
    lat_n, lon_n = lax.axis_size("lat"), lax.axis_size("lon")
    assert lat_n > 1 and lat_n & (lat_n - 1) == 0

    place = np.zeros((total, channels), np.float32)
    for at, c in enumerate(order):
        place[at, c] = 1.0
    scatter = np.zeros((channels, kept), np.float32)
    for at, c in enumerate(order[:scored]):
        scatter[c, at] = 1.0
    shift = np.zeros((noise, total), np.float32)
    for k in range(noise):
        shift[k, state_rows + k] = 1.0
    place, placed, scatter, shift = (jnp.asarray(x, BF16) for x in (place, place.T, scatter, shift))
    sources = [
        input_weight.T, random_weight.T, hidden_weight, output_weight, diffusivity.reshape(1, channels),
        place, placed, scatter, shift,
    ]

    whole2 = lambda shape: pl.BlockSpec(shape, lambda *_: (0,) * len(shape))

    rows_t, low, high, edge, w_in, w_in_half, w_mid_half, w_out, w_out_half, coef = pl.pallas_call(
        functools.partial(transpose_kernel, order, channels, len(sources)),
        grid=(members, blocks),
        in_specs=[
            pl.BlockSpec((1, channels, SUB, lanes), lambda m, r: (m, 0, r, 0)),
            pl.BlockSpec((1, noise, SUB, lanes), lambda m, r: (m, 0, r, 0)),
            *[whole2(x.shape) for x in sources],
        ],
        out_specs=[RESIDENT] * 10,
        out_shape=[
            pltpu.VMEM((members, lat_rows, total, lanes), F32),
            pltpu.VMEM((members, state_rows, lanes), BF16),
            pltpu.VMEM((members, state_rows, lanes), BF16),
            pltpu.VMEM((state_rows, lanes), BF16),
            pltpu.VMEM((hidden, total), BF16),
            pltpu.VMEM((hidden, total), BF16),
            pltpu.VMEM((hidden, hidden), BF16),
            pltpu.VMEM((kept, hidden), BF16),
            pltpu.VMEM((kept, hidden), BF16),
            pltpu.VMEM((state_rows, lanes), F32),
        ],
        scratch_shapes=[
            pltpu.VMEM((total * SUB, lanes), F32),
            pltpu.VMEM((state_rows, lanes), F32),
        ],
        compiler_params=params(),
        name="transpose",
    )(in_hbm(starting_state), in_hbm(random_fields), *map(in_hbm, sources))
    sides = [lax.ppermute(edge, "lon", ring("lon", k)) for k in (1, -1)]

    target = pl.pallas_call(
        functools.partial(observed_kernel, scored),
        in_specs=[RESIDENT],
        out_specs=RESIDENT,
        out_shape=pltpu.VMEM((lat_rows, kept, lanes), F32),
        scratch_shapes=[pltpu.VMEM((kept * SUB, lanes), F32)],
        compiler_params=params(),
        name="observed",
    )(in_vmem(observed.reshape(scored, lat_rows, lanes)))

    half = SUB // 2
    inner = [(at, SUB) for at in range(SUB, lat_rows - SUB, SUB)]
    pieces = [*inner, (0, SUB), (lat_rows - half, half), (lat_rows - SUB, half)]

    def forward(index, swapped, sides):
        first_row, chunk = pieces[index]
        cells = chunk * lanes
        at_start, at_end = first_row == 0, first_row + chunk == lat_rows
        halo = list(swapped) if at_start or at_end else []

        def body(t_ref, *refs):
            got, refs = refs[: len(halo)], refs[len(halo) :]
            up, down = got if at_start else None, got if at_end else None
            around, weights, *refs = refs
            if index == 0:
                left, right, (around, weights, keep) = around, weights, refs[-3:]
                stencil_setup(left, right, around, weights)
                refs = [*refs[:-3], keep]
            forward_kernel(first_row, chunk, scored, span, t_ref, up, down, around, weights, *refs)

        return pl.pallas_call(
            body,
            in_specs=[RESIDENT] * (7 + len(halo)),
            out_specs=[RESIDENT] * (9 if index == 0 else 7),
            out_shape=[
                pltpu.VMEM((members, chunk, kept, lanes), BF16),
                pltpu.VMEM((members, total, cells), BF16),
                pltpu.VMEM((members, chunk, state_rows, lanes), BF16),
                *[pltpu.VMEM((members, hidden, cells), BF16) for _ in range(4)],
                *([pltpu.VMEM((state_rows, lanes), F32)] if index == 0 else []),
                *([pltpu.VMEM((2 * lanes, lanes), BF16)] if index == 0 else []),
            ],
            scratch_shapes=[pltpu.VMEM((kept, cells), F32)],
            compiler_params=params(),
        )(in_vmem(rows_t), *halo, *map(in_vmem, sides), coef, w_in_half, w_mid_half, w_out)

    pack_rows = round_up(total + hidden + kept + 8, 16 * lat_n)

    def backward(index, residuals, others, carried, grads):
        own, x, lap, act1, slope1, act2, slope2 = residuals
        first, last = index == 0, index == len(pieces) - 1
        first_row = pieces[index][0]
        rows = 4
        accs = [(total, hidden), (hidden, hidden), (kept, hidden), (state_rows, lanes), (state_rows, lanes)]
        acc_types = [F32, F32, F32, F32, BF16]
        inputs = [
            *map(in_vmem, (own, *others, target, x, lap, act1, slope1, act2, slope2)),
            w_in, w_mid_half, w_out_half, *map(in_vmem, carried), *([] if first else [in_vmem(grads)]),
        ]
        outputs = [
            pltpu.VMEM((members, lat_rows, state_rows, lanes), F32),
            *[pltpu.VMEM(shape, kind) for shape, kind in zip(accs, acc_types, strict=True)],
            *([pltpu.VMEM((members, state_rows, lanes), BF16)] * 2 if last else []),
            *([pltpu.VMEM((pack_rows // 2, hidden), BF16)] * 2 if last else []),
        ]
        return pl.pallas_call(
            functools.partial(backward_kernel, partners, first, last, first_row, span),
            in_specs=[RESIDENT] * len(inputs),
            out_specs=[RESIDENT] * len(outputs),
            out_shape=outputs,
            input_output_aliases={} if first else {len(inputs) - 1: 0},
            scratch_shapes=[
                *([pltpu.VMEM((pack_rows, hidden), BF16)] if last else []),
                pltpu.VMEM((members, kept, rows * lanes), BF16),
                pltpu.VMEM((state_rows, lanes), F32),
            ],
            compiler_params=params(),
        )(*inputs)

    saved, received = {}, {}
    swapped = None
    for index in range(len(pieces)):
        if index == len(inner):
            swapped = swap(low, 0), swap(high, 1)
        saved[index] = forward(index, swapped, sides)
        if index == 0:
            *saved[index], around, turned = saved[index]
            sides = around, turned
        received[index] = [
            lax.ppermute(saved[index][0], "ens", ring("ens", k)) for k in range(1, partners + 1)
        ]
    grads, carried = None, []
    for index in range(len(pieces)):
        grads, *carried = backward(index, saved[index], received[index], carried, grads)
        carried, more = carried[:5], carried[5:]
    edge, (low, high, mine, other) = carried[-1], more
    first = swap(low, 0)
    swapped = first, swap(high, 1)
    left = lax.ppermute(edge, "lon", ring("lon", 1))
    sides = left, lax.ppermute(edge, "lon", ring("lon", -1))

    def final(which, out):
        inputs = [*map(in_vmem, (grads, *swapped, *sides)), coef]
        first, stride = which[0], which[1] - which[0]
        index_map = lambda m, j: (m, 0, first + j * stride, 0)
        return pl.pallas_call(
            functools.partial(final_kernel, order, span, SUB, first, stride, blocks),
            grid=(members, len(which)),
            in_specs=[
                *[RESIDENT] * len(inputs),
                *([] if out is None else [pl.BlockSpec(memory_space=pl.ANY)]),
            ],
            out_specs=pl.BlockSpec((1, channels, SUB, lanes), index_map),
            out_shape=pltpu.HBM(starting_state.shape, BF16),
            scratch_shapes=[
                pltpu.VMEM((state_rows * SUB, lanes), F32),
                pltpu.VMEM((state_rows, lanes), F32),
                pltpu.VMEM((2 * lanes, lanes), BF16),
            ],
            input_output_aliases={} if out is None else {len(inputs): 0},
            compiler_params=params(),
            name="final",
        )(*inputs, *([] if out is None else [out]))

    bits = [1 << k for k in range(lat_n.bit_length() - 1)]
    for bit in bits:
        parts = [mine, across(other, bit)]
        parts = add_parts(parts, None if bit == bits[-1] else 2 * bit)
        mine, other = parts[0], parts[-1]
    parts = everyone(mine, "ens")
    (mine,) = add_parts(parts)
    parts = everyone(mine, "lon")
    grad_state = final(range(1, blocks - 1), None)
    (mine,) = add_parts(parts)
    for bit in bits[::-1]:
        other = across(mine, bit)
        if bit != bits[0]:
            mine = join(bit, mine, other)
    parts = [mine, other]
    grad_state = final((0, blocks - 1), grad_state)
    count = members * (partners + 1) * lat_rows * lat_n * lanes * lon_n
    g_in, g_noise, g_mid, g_out, g_diff = pl.pallas_call(
        functools.partial(unpack_kernel, channels, noise, 1.0 / count),
        out_shape=[
            jax.ShapeDtypeStruct((channels, hidden), F32),
            jax.ShapeDtypeStruct((noise, hidden), F32),
            jax.ShapeDtypeStruct((hidden, hidden), F32),
            jax.ShapeDtypeStruct((channels, hidden), F32),
            jax.ShapeDtypeStruct((1, channels), F32),
        ],
        scratch_shapes=[pltpu.VMEM((pack_rows, hidden), BF16)],
        compiler_params=params(),
        name="unpack",
    )(*map(in_vmem, parts), place, scatter)
    return grad_state, g_in.T, g_noise.T, g_mid, g_out, g_diff.reshape(channels)


def solution(mesh):
    tiles = P("ens", None, "lat", "lon")
    in_specs = (tiles, tiles, P(None, None, "lat", "lon"), P(), P(), P(), P(), P())
    out_specs = (tiles, P(), P(), P(), P(), P())

    return jax.shard_map(on_device, mesh=mesh, in_specs=in_specs, out_specs=out_specs, check_vma=False)
```
